128 devices in a mesh: row: 16 (over x, y_lo, core), col: 8 (over y_hi, z).
Axes of the slice: x: 4, y: 4 (y_hi: 2, y_lo: 2; y = y_hi * 2 + y_lo), z: 4, core: 2. Of those that a mesh axis runs over, the one named last changes fastest.
Arguments:
- cooccur: bfloat16 [16384, 65536], P('row', 'col'), as said below
- anchors: int32 [256], replicated, may hold values from 0 to 16383, as said below
Outputs:
- weights: float32 [256, 16384], P(None, ('row', 'col'))
The draws below stay inside these ranges and needn't reach their ends.
Inputs may be any that keep to these rules, and one draw needn't show every extreme that they name: `anchors`: 256 distinct indices of rows of cooccur. `cooccur`: all entries are positive.
All inputs are finite; a program needn't handle non-finite values.
Results may differ from the reference program's by a relative error of at most 0.0005.
Values may be sent and summed in bfloat16 or wider, within the bound.
No kernel may reach another device: no remote copies, remote signals or barrier semaphores. Data moves between devices by JAX's collectives and lax.ppermute only.
A program may use at most 128 MiB of HBM per device.

```python
import math
import jax
import jax.numpy as jnp
from jax import lax

VOCAB = 65536
ANCHORS = 256
BLOCK = 32
SWEEPS = 2
ROWS_DEV = 1024
WORDS = 16384


def draw_cooccur(key, part):
    key_rows = jax.random.fold_in(key, 0)
    key_cols = jax.random.fold_in(key, 1)
    key_cells = jax.random.fold_in(key, 2)
    key_groups = jax.random.fold_in(key, 4)
    row_scale = jnp.exp(jax.random.uniform(key_rows, (WORDS, 1), jnp.float32, 0.0, math.log(10.0)))
    ramp = jnp.arange(VOCAB, dtype=jnp.float32)[None, :] / VOCAB
    col_scale = jnp.exp(ramp * math.log(10.0) + jax.random.uniform(key_cols, (1, VOCAB), jnp.float32, -0.4, 0.4))
    group_count = 16
    group_weight = jnp.exp(jax.random.uniform(key_groups, (WORDS, group_count, 1), jnp.float32, -1.5, 1.5))
    profile = jnp.broadcast_to(group_weight, (WORDS, group_count, VOCAB // group_count)).reshape(WORDS, VOCAB)
    base = jax.random.uniform(key_cells, (WORDS, VOCAB), jnp.float32, 0.1, 1.0)
    return (row_scale * col_scale * profile * base).astype(jnp.bfloat16)


def draw_anchors(key, part):
    shuffled = jax.random.permutation(key, WORDS - 2) + 1
    chosen = jnp.concatenate([jnp.array([0, WORDS - 1], jnp.int32), shuffled[:ANCHORS - 2].astype(jnp.int32)])
    order = jax.random.permutation(jax.random.fold_in(key, 7), ANCHORS)
    return chosen[order].astype(jnp.int32)


def setup_inputs(seed: int = 0) -> dict:
    arg_keys = jax.random.split(jax.random.key(seed), 3)
    return {
        "cooccur": draw_cooccur(jax.random.fold_in(arg_keys[2], 71), 0),
        "anchors": draw_anchors(jax.random.fold_in(arg_keys[2], 71), 0),
    }


def hals_sweeps(projected_t, gram_matrix):
    coef = jnp.full(projected_t.shape, 1.0 / ANCHORS, jnp.float32)
    for sweep_index in range(SWEEPS):
        for block_index in range(ANCHORS // BLOCK):
            block_start = block_index * BLOCK
            gram_cols = gram_matrix[:, block_start:block_start + BLOCK]
            resid = projected_t[block_start:block_start + BLOCK] - jnp.dot(gram_cols.T, coef, precision=lax.Precision.HIGHEST)
            gram_block = gram_matrix[block_start:block_start + BLOCK, block_start:block_start + BLOCK]
            row_list = [coef[block_start + position] for position in range(BLOCK)]
            for position in range(BLOCK):
                old_value = row_list[position]
                new_value = jnp.maximum(old_value + resid[position] / gram_block[position, position], 0.0)
                delta = new_value - old_value
                row_list[position] = new_value
                resid = resid - gram_block[:, position][:, None] * delta[None, :]
            coef = jnp.concatenate([coef[:block_start], jnp.stack(row_list, axis=0), coef[block_start + BLOCK:]], axis=0)
    return coef


def reference(cooccur, anchors):
    raw_rows = jnp.take(cooccur, anchors, axis=0)
    anchor_totals = jnp.sum(raw_rows.astype(jnp.float32), axis=1)
    anchor_basis = (raw_rows.astype(jnp.float32) / anchor_totals[:, None]).astype(jnp.bfloat16)
    gram_matrix = jnp.dot(anchor_basis, anchor_basis.T, preferred_element_type=jnp.float32)

    def per_block(block_rows):
        block_totals = jnp.sum(block_rows.astype(jnp.float32), axis=1)
        product = jnp.dot(block_rows, anchor_basis.T, preferred_element_type=jnp.float32)
        return product / block_totals[:, None]

    blocks = cooccur.reshape(WORDS // ROWS_DEV, ROWS_DEV, VOCAB)
    projected = lax.map(per_block, blocks).reshape(WORDS, ANCHORS)
    coef = hals_sweeps(projected.T, gram_matrix)
    return ANCHORS * coef
```

```python
import functools

import jax
import jax.numpy as jnp
from jax import lax
from jax.experimental import pallas as pl
from jax.experimental.pallas import tpu as pltpu
from jax.sharding import PartitionSpec as P

ANCHORS = 256
BLOCK = 32
SWEEPS = 2
BLOCKS = ANCHORS // BLOCK
TILE = 1024
SLOTS = 32
XS, YS, CORES = 4, 2, 2
SOURCES = XS * YS * CORES


def shifted(dx, dy, dc):
    moves = []
    for x in range(XS):
        for y in range(YS):
            for c in range(CORES):
                source = (x * YS + y) * CORES + c
                target = (((x + dx) % XS) * YS + (y ^ dy)) * CORES + (c ^ dc)
                moves.append((source, target))
    return moves


def send(value, dx, dy, dc=0):
    return lax.ppermute(value, "row", shifted(dx, dy, dc))


def spread_row(ref, row):
    return ref[pl.ds(row, 8, stride=0), :]


def hals_kernel(proj_ref, tot_ref, gram_ref, out_ref, target, coef, ratio, work, inverse):
    words = out_ref.shape[1]
    target[...] = (proj_ref[...] / tot_ref[...]).T
    coef[...] = jnp.full_like(coef, 1.0 / ANCHORS)
    row_id = lax.broadcasted_iota(jnp.int32, (BLOCK, BLOCK), 0)
    col_id = lax.broadcasted_iota(jnp.int32, (BLOCK, BLOCK), 1)
    for block in range(BLOCKS):
        start = block * BLOCK
        square = gram_ref[start : start + BLOCK, start : start + BLOCK]
        diagonal = jnp.sum(jnp.where(row_id == col_id, square, 0.0), axis=1, keepdims=True)
        inv = 1.0 / diagonal
        inverse[start : start + BLOCK, :] = jnp.broadcast_to(inv, (BLOCK, words))
        scaled = square * inv
        for j in range(BLOCK):
            first = start * BLOCK + j * BLOCK
            ratio[first : first + BLOCK, :] = jnp.broadcast_to(
                scaled[:, j : j + 1], (BLOCK, words)
            )

    def step(index, carry):
        block = lax.rem(index, BLOCKS)
        start = pl.multiple_of(block * BLOCK, BLOCK)
        rows = pl.ds(start, BLOCK)
        moved = jnp.dot(
            gram_ref[rows, :],
            coef[...],
            precision=lax.Precision.HIGHEST,
            preferred_element_type=jnp.float32,
        )
        work[...] = (target[rows, :] - moved) * inverse[rows, :]
        resid = [spread_row(work, m) for m in range(BLOCK)]
        base = start * BLOCK
        for j in range(BLOCK):
            old = spread_row(coef, start + j)
            delta = jnp.maximum(resid[j], -old)
            coef[pl.ds(start + j, 1), :] = (old + delta)[0:1, :]
            for m in range(j + 1, BLOCK):
                resid[m] = resid[m] - spread_row(ratio, base + j * BLOCK + m) * delta
        return carry

    lax.fori_loop(0, SWEEPS * BLOCKS, step, 0)
    out_ref[...] = ANCHORS * coef[...]


def hals(projected, totals, gram):
    words = projected.shape[0]
    return pl.pallas_call(
        hals_kernel,
        out_shape=jax.ShapeDtypeStruct((ANCHORS, words), jnp.float32),
        scratch_shapes=[
            pltpu.VMEM((ANCHORS, words), jnp.float32),
            pltpu.VMEM((ANCHORS, words), jnp.float32),
            pltpu.VMEM((ANCHORS * BLOCK, words), jnp.float32),
            pltpu.VMEM((BLOCK, words), jnp.float32),
            pltpu.VMEM((ANCHORS, words), jnp.float32),
        ],
        compiler_params=pltpu.CompilerParams(vmem_limit_bytes=32 << 20),
        name="hals",
    )(projected, totals, gram)


def product_kernel(layout, tiles, totals_ref, place_ref, block_ref, *rest):
    piece_count = len(rest) - 6
    pieces = rest[:piece_count]
    proj_ref, gram_ref, held, sems, select, scale = rest[piece_count:]
    tile = pl.program_id(0)

    def copies(index):
        found = []
        for source in range(SOURCES):
            piece, offset = layout[source][index]
            found.append(
                pltpu.make_async_copy(
                    pieces[piece].at[:, pl.ds(offset, TILE)],
                    held.at[index, pl.ds(source * SLOTS, SLOTS), :],
                    sems.at[index, source],
                )
            )
        return found

    @pl.when(tile == 0)
    def _():
        for index in range(tiles):
            for copy in copies(index):
                copy.start()
        slot = lax.broadcasted_iota(jnp.int32, (ANCHORS, SOURCES * SLOTS), 1)
        chosen = slot == place_ref[...]
        select[...] = chosen.astype(jnp.float32).astype(jnp.bfloat16)
        scale[...] = 1.0 / jnp.sum(jnp.where(chosen, totals_ref[...], 0.0), axis=1, keepdims=True)
        proj_ref[...] = jnp.zeros_like(proj_ref)
        gram_ref[...] = jnp.zeros_like(gram_ref)

    for index in range(tiles):

        @pl.when(tile == index)
        def _(index=index):
            for copy in copies(index):
                copy.wait()

    raw = jnp.dot(select[...], held[tile], preferred_element_type=jnp.float32)
    basis = (raw * scale[...]).astype(jnp.bfloat16)
    contract = (((1,), (1,)), ((), ()))
    gram_ref[...] += lax.dot_general(basis, basis, contract, preferred_element_type=jnp.float32)
    proj_ref[...] += lax.dot_general(
        block_ref[...], basis, contract, preferred_element_type=jnp.float32
    )


def products(cooccur, pieces, layout, slot_totals, place):
    rows, columns = cooccur.shape
    tiles = columns // TILE
    return pl.pallas_call(
        functools.partial(product_kernel, layout, tiles),
        grid=(tiles,),
        in_specs=[
            pl.BlockSpec((1, SOURCES * SLOTS), lambda i: (0, 0)),
            pl.BlockSpec((ANCHORS, 1), lambda i: (0, 0)),
            pl.BlockSpec((rows, TILE), lambda i: (0, i)),
        ]
        + [pl.BlockSpec(memory_space=pl.ANY)] * len(pieces),
        out_specs=[
            pl.BlockSpec((rows, ANCHORS), lambda i: (0, 0)),
            pl.BlockSpec((ANCHORS, ANCHORS), lambda i: (0, 0)),
        ],
        out_shape=[
            jax.ShapeDtypeStruct((rows, ANCHORS), jnp.float32),
            jax.ShapeDtypeStruct((ANCHORS, ANCHORS), jnp.float32),
        ],
        scratch_shapes=[
            pltpu.VMEM((tiles, SOURCES * SLOTS, TILE), jnp.bfloat16),
            pltpu.SemaphoreType.DMA((tiles, SOURCES)),
            pltpu.VMEM((ANCHORS, SOURCES * SLOTS), jnp.bfloat16),
            pltpu.VMEM((ANCHORS, 1), jnp.float32),
        ],
        compiler_params=pltpu.CompilerParams(
            dimension_semantics=("arbitrary",), vmem_limit_bytes=48 << 20
        ),
        name="products",
    )(slot_totals, place, cooccur, *pieces)


def exchange(own):
    columns = own.shape[1]
    tiles = columns // TILE
    half = tiles // 2
    first, last = (3 * tiles) // 8, (5 * tiles) // 8
    cut = lambda value, start, stop: value[:, start * TILE : stop * TILE]
    left = send(own, 1, 0)
    right = send(own, -1, 0)
    across = send(own, 0, 1)
    far_lo = send(cut(left, 0, half), 1, 0)
    far_hi = send(cut(right, half, tiles), -1, 0)
    across_left_lo = send(cut(across, 0, half), 1, 0)
    across_right_lo = send(cut(across, 0, half), -1, 0)
    across_left_hi = send(cut(left, half, tiles), 0, 1)
    across_right_hi = send(cut(right, half, tiles), 0, 1)
    beyond_a = send(cut(across_left_lo, 0, first), 1, 0)
    beyond_b = send(cut(far_lo, first, half), 0, 1)
    beyond_c = send(cut(far_hi, 0, last - half), 0, 1)
    beyond_d = send(cut(across_right_hi, last - half, half), -1, 0)
    table = {
        (0, 0): [(own, 0, tiles)],
        (1, 0): [(left, 0, tiles)],
        (3, 0): [(right, 0, tiles)],
        (0, 1): [(across, 0, tiles)],
        (2, 0): [(far_lo, 0, half), (far_hi, half, tiles)],
        (1, 1): [(across_left_lo, 0, half), (across_left_hi, half, tiles)],
        (3, 1): [(across_right_lo, 0, half), (across_right_hi, half, tiles)],
        (2, 1): [
            (beyond_a, 0, first),
            (beyond_b, first, half),
            (beyond_c, half, last),
            (beyond_d, last, tiles),
        ],
    }
    pieces, layout = [], []
    for dc in range(CORES):
        for dx in range(XS):
            for dy in range(YS):
                spots = [None] * tiles
                for value, start, stop in table[dx, dy]:
                    pieces.append(send(value, 0, 0, 1) if dc else value)
                    for tile in range(start, stop):
                        spots[tile] = (len(pieces) - 1, (tile - start) * TILE)
                layout.append(spots)
    return pieces, layout


def sum_shares(value):
    return jnp.sum(lax.all_to_all(value, "col", 0, 0), axis=0)


def gathered(value, axis):
    size = lax.axis_size(axis)
    return lax.all_to_all(jnp.broadcast_to(value[None], (size,) + value.shape), axis, 0, 0)


def finish(proj, gram, totals):
    share = proj.shape[0] // lax.axis_size("col")
    gram_share = sum_shares(gram.reshape(-1, ANCHORS // lax.axis_size("col"), ANCHORS))
    gram_matrix = gathered(gram_share, "col").reshape(ANCHORS, ANCHORS)
    projected = sum_shares(proj.reshape(-1, share, ANCHORS))
    own_totals = sum_shares(totals.reshape(-1, share))
    return hals(projected, own_totals[:, None], gram_matrix)


def quick(cooccur, anchors, owner, rank):
    rows = cooccur.shape[0]
    me = lax.axis_index("row")
    mine = (owner == me)[None, :] & (rank[None, :] == jnp.arange(SLOTS)[:, None])
    local = jnp.sum(jnp.where(mine, (anchors % rows)[None, :], 0), axis=1)
    own = jnp.take(cooccur, local, axis=0)
    pieces, layout = exchange(own)
    own_sums = jnp.sum(own.astype(jnp.float32), axis=1)
    slot_sums = lax.psum(own_sums, "col")
    slot_totals = gathered(slot_sums, "row")
    sources = jnp.arange(SOURCES)
    dc, dx, dy = sources // (XS * YS), sources // YS % XS, sources % YS
    mx, my, mc = me // (YS * CORES), me // CORES % YS, me % CORES
    absolute = (((mx - dx) % XS) * YS + (my ^ dy)) * CORES + (mc ^ dc)
    pick = absolute[:, None] == jnp.arange(SOURCES)[None, :]
    slot_totals = jnp.sum(jnp.where(pick[:, :, None], slot_totals[None], 0.0), axis=1)
    ox, oy, oc = owner // (YS * CORES), owner // CORES % YS, owner % CORES
    relative = ((mc ^ oc) * XS + (mx - ox) % XS) * YS + (my ^ oy)
    place = relative * SLOTS + rank
    totals = jnp.sum(cooccur, axis=1, dtype=jnp.float32)
    proj, gram = products(
        cooccur, pieces, layout, slot_totals.reshape(1, -1), place[:, None].astype(jnp.int32)
    )
    return finish(proj, gram, totals)


def general(cooccur, anchors, owner, rank):
    rows = cooccur.shape[0]
    inside = owner == lax.axis_index("row")
    local = jnp.where(inside, anchors % rows, 0)
    picked = jnp.take(cooccur, local, axis=0)
    payload = jnp.where(inside[:, None], picked, jnp.zeros_like(picked))
    raw = lax.psum(payload, "row").astype(jnp.float32)
    scale = lax.psum(jnp.sum(raw, axis=1), "col")
    basis = (raw / scale[:, None]).astype(jnp.bfloat16)
    gram = jnp.dot(basis, basis.T, preferred_element_type=jnp.float32)
    proj = jnp.dot(cooccur, basis.T, preferred_element_type=jnp.float32)
    totals = jnp.sum(cooccur, axis=1, dtype=jnp.float32)
    return finish(proj, gram, totals)


def per_device(cooccur, anchors):
    rows = cooccur.shape[0]
    owner = anchors // rows
    earlier = jnp.arange(ANCHORS)[None, :] < jnp.arange(ANCHORS)[:, None]
    rank = jnp.sum((owner[:, None] == owner[None, :]) & earlier, axis=1)
    return lax.cond(jnp.max(rank) < SLOTS, quick, general, cooccur, anchors, owner, rank)


def solution(mesh):
    placed = (P("row", "col"), P())
    return jax.shard_map(
        per_device, mesh=mesh, in_specs=placed, out_specs=P(None, ("row", "col")), check_vma=False
    )
```

```python
import jax
import jax.numpy as jnp
from jax import lax
from jax.experimental import pallas as pl
from jax.experimental.pallas import tpu as pltpu
from jax.sharding import PartitionSpec as P

ANCHORS = 256
BLOCK = 32
SWEEPS = 2
BLOCKS = ANCHORS // BLOCK
TILE = 1024
WIDE = 2048
SLOTS = 32
XS, YS, CORES = 4, 2, 2
SOURCES = XS * YS * CORES
SHIFTS = [(0, 0), (1, 0), (-1, 0), (0, 1), (2, 1), (2, 0), (1, 1), (-1, 1)]
GROUP = 8
EXTRA = 8
CONTRACT = (((1,), (1,)), ((), ()))


def shifted(dx, dy, dc):
    moves = []
    for x in range(XS):
        for y in range(YS):
            for c in range(CORES):
                source = (x * YS + y) * CORES + c
                target = (((x + dx) % XS) * YS + (y ^ dy)) * CORES + (c ^ dc)
                moves.append((source, target))
    return moves


def send(value, dx, dy, dc=0):
    return lax.ppermute(value, "row", shifted(dx, dy, dc))


def spread_row(ref, row):
    return ref[pl.ds(row, 8, stride=0), :]


def hals_kernel(share_ref, gram_in_ref, out_ref, gram_ref, target, coef, ratio, work, inverse):
    words = out_ref.shape[1]
    gram_ref[...] = gram_in_ref[...].reshape(ANCHORS, ANCHORS)
    share = jnp.sum(share_ref[...], axis=0)
    last = share.shape[0] - 1
    target[...] = share[:words, :].T / share[last:, :words]
    coef[...] = jnp.full_like(coef, 1.0 / ANCHORS)
    row_id = lax.broadcasted_iota(jnp.int32, (BLOCK, BLOCK), 0)
    col_id = lax.broadcasted_iota(jnp.int32, (BLOCK, BLOCK), 1)
    for block in range(BLOCKS):
        start = block * BLOCK
        square = gram_ref[start : start + BLOCK, start : start + BLOCK]
        diagonal = jnp.sum(jnp.where(row_id == col_id, square, 0.0), axis=1, keepdims=True)
        inv = 1.0 / diagonal
        inverse[start : start + BLOCK, :] = jnp.broadcast_to(inv, (BLOCK, words))
        scaled = square * inv
        for j in range(BLOCK):
            first = start * BLOCK + j * BLOCK
            ratio[first : first + BLOCK, :] = jnp.broadcast_to(
                scaled[:, j : j + 1], (BLOCK, words)
            )

    def step(index, carry):
        block = lax.rem(index, BLOCKS)
        start = pl.multiple_of(block * BLOCK, BLOCK)
        rows = pl.ds(start, BLOCK)
        moved = jnp.dot(
            gram_ref[rows, :],
            coef[...],
            precision=lax.Precision.HIGHEST,
            preferred_element_type=jnp.float32,
        )
        work[...] = (target[rows, :] - moved) * inverse[rows, :]
        resid = [spread_row(work, m) for m in range(BLOCK)]
        base = start * BLOCK
        for j in range(BLOCK):
            old = spread_row(coef, start + j)
            delta = jnp.maximum(resid[j], -old)
            coef[pl.ds(start + j, 1), :] = (old + delta)[0:1, :]
            for m in range(j + 1, BLOCK):
                resid[m] = resid[m] - spread_row(ratio, base + j * BLOCK + m) * delta
        return carry

    lax.fori_loop(0, SWEEPS * BLOCKS, step, 0)
    out_ref[...] = ANCHORS * coef[...]


def hals(shares, gram):
    words = shares.shape[1] - EXTRA - gram.shape[1]
    return pl.pallas_call(
        hals_kernel,
        out_shape=jax.ShapeDtypeStruct((ANCHORS, words), jnp.float32),
        scratch_shapes=[
            pltpu.VMEM((ANCHORS, ANCHORS), jnp.float32),
            pltpu.VMEM((ANCHORS, words), jnp.float32),
            pltpu.VMEM((ANCHORS, words), jnp.float32),
            pltpu.VMEM((ANCHORS * BLOCK, words), jnp.float32),
            pltpu.VMEM((BLOCK, words), jnp.float32),
            pltpu.VMEM((ANCHORS, words), jnp.float32),
        ],
        compiler_params=pltpu.CompilerParams(vmem_limit_bytes=32 << 20),
        name="hals",
    )(shares, gram)


def pick_kernel(group_ref, spot_ref, block_ref, own_ref, sums_ref, held, sems):
    columns = block_ref.shape[1]
    copies = []
    for slot in range(SLOTS):
        first = pl.multiple_of(group_ref[slot] * GROUP, GROUP)
        copies.append(
            pltpu.make_async_copy(
                block_ref.at[pl.ds(first, GROUP), :],
                held.at[pl.ds(slot * GROUP, GROUP), :],
                sems.at[slot],
            )
        )
        copies[-1].start()
    row = lax.broadcasted_iota(jnp.int32, (SLOTS, SLOTS * GROUP), 1)
    select = (row == spot_ref[...]).astype(jnp.float32).astype(jnp.bfloat16)
    for copy in copies:
        copy.wait()
    sums = jnp.zeros((SLOTS, 1), jnp.float32)
    for start in range(0, columns, TILE):
        rows = jnp.dot(
            select, held[:, start : start + TILE], preferred_element_type=jnp.float32
        )
        own_ref[:, start : start + TILE] = rows.astype(jnp.bfloat16)
        sums = sums + jnp.sum(rows, axis=1, keepdims=True)
    sums_ref[...] = sums


def pick(cooccur, local):
    columns = cooccur.shape[1]
    spot = jnp.arange(SLOTS) * GROUP + local % GROUP
    return pl.pallas_call(
        pick_kernel,
        grid_spec=pltpu.PrefetchScalarGridSpec(
            num_scalar_prefetch=1,
            grid=(1,),
            in_specs=[
                pl.BlockSpec((SLOTS, 1), lambda i, g: (0, 0)),
                pl.BlockSpec(memory_space=pltpu.HBM),
            ],
            out_specs=[
                pl.BlockSpec((SLOTS, columns), lambda i, g: (0, 0)),
                pl.BlockSpec((SLOTS, 1), lambda i, g: (0, 0)),
            ],
            scratch_shapes=[
                pltpu.VMEM((SLOTS * GROUP, columns), jnp.bfloat16),
                pltpu.SemaphoreType.DMA((SLOTS,)),
            ],
        ),
        out_shape=[
            jax.ShapeDtypeStruct((SLOTS, columns), jnp.bfloat16),
            jax.ShapeDtypeStruct((SLOTS, 1), jnp.float32),
        ],
        compiler_params=pltpu.CompilerParams(vmem_limit_bytes=24 << 20),
        cost_estimate=pl.CostEstimate(
            flops=0, bytes_accessed=SLOTS * GROUP * columns * 2, transcendentals=0
        ),
        name="pick",
    )((local // GROUP).astype(jnp.int32), spot[:, None].astype(jnp.int32), cooccur)


def products_kernel(totals_ref, place_ref, sums_ref, block_ref, *rest):
    piece_count = len(rest) - 7
    pieces = rest[:piece_count]
    out_ref, held, block, proj, gram_sum, held_sems, block_sems = rest[piece_count:]
    tiles = held.shape[0]
    parts, rows = out_ref.shape[0], out_ref.shape[1] - EXTRA
    gram_rows = ANCHORS // parts
    rows -= gram_rows
    found, fetched = [], []
    for tile in range(tiles):
        start = 0
        for index, piece in enumerate(pieces):
            split = piece.shape[1] < tiles * WIDE
            size = piece.shape[0] // 2 if split else piece.shape[0]
            row, column = divmod(tile * WIDE, piece.shape[1])
            found.append(
                pltpu.make_async_copy(
                    piece.at[pl.ds(row * size, size), pl.ds(column, WIDE)],
                    held.at[tile, pl.ds(start, size), :],
                    held_sems.at[tile, index],
                )
            )
            found[-1].start()
            start += size
        fetched.append(
            pltpu.make_async_copy(
                block_ref.at[:, pl.ds(tile * WIDE, WIDE)], block.at[tile], block_sems.at[tile]
            )
        )
        fetched[-1].start()
    slot = lax.broadcasted_iota(jnp.int32, (ANCHORS, SOURCES * SLOTS), 1)
    chosen = slot == place_ref[...]
    select = chosen.astype(jnp.float32).astype(jnp.bfloat16)
    scale = 1.0 / jnp.sum(jnp.where(chosen, totals_ref[...], 0.0), axis=1, keepdims=True)
    for tile in range(tiles):
        for copy in found[tile * piece_count : (tile + 1) * piece_count]:
            copy.wait()
        raw = jnp.dot(select, held[tile], preferred_element_type=jnp.float32)
        basis = (raw * scale).astype(jnp.bfloat16)
        gram = lax.dot_general(basis, basis, CONTRACT, preferred_element_type=jnp.float32)
        fetched[tile].wait()
        product = lax.dot_general(
            block[tile], basis, CONTRACT, preferred_element_type=jnp.float32
        )
        if tile == 0:
            gram_sum[...] = gram
            proj[...] = product
        else:
            gram_sum[...] += gram
            proj[...] += product
    for part in range(parts):
        out_ref[part, :rows, :] = proj[part * rows : (part + 1) * rows, :]
        out_ref[part, rows : rows + gram_rows, :] = gram_sum[
            part * gram_rows : (part + 1) * gram_rows, :
        ]
        row = jnp.concatenate([sums_ref[part : part + 1, :]] * (ANCHORS // rows), axis=1)
        out_ref[part, rows + gram_rows :, :] = jnp.broadcast_to(row, (EXTRA, ANCHORS))


def products(cooccur, pieces, slot_totals, place, sums):
    rows, columns = cooccur.shape
    parts = sums.shape[0]
    tiles = columns // WIDE
    return pl.pallas_call(
        products_kernel,
        in_specs=[pl.BlockSpec(memory_space=pltpu.VMEM)] * 3
        + [pl.BlockSpec(memory_space=pltpu.HBM)] * (1 + len(pieces)),
        out_specs=pl.BlockSpec(memory_space=pltpu.VMEM),
        out_shape=jax.ShapeDtypeStruct(
            (parts, (rows + ANCHORS) // parts + EXTRA, ANCHORS), jnp.float32
        ),
        scratch_shapes=[
            pltpu.VMEM((tiles, SOURCES * SLOTS, WIDE), jnp.bfloat16),
            pltpu.VMEM((tiles, rows, WIDE), jnp.bfloat16),
            pltpu.VMEM((rows, ANCHORS), jnp.float32),
            pltpu.VMEM((ANCHORS, ANCHORS), jnp.float32),
            pltpu.SemaphoreType.DMA((tiles, len(pieces))),
            pltpu.SemaphoreType.DMA((tiles,)),
        ],
        compiler_params=pltpu.CompilerParams(vmem_limit_bytes=52 << 20),
        cost_estimate=pl.CostEstimate(
            flops=2 * ANCHORS * (SOURCES * SLOTS + ANCHORS + rows) * columns,
            bytes_accessed=(SOURCES * SLOTS + rows) * columns * 2,
            transcendentals=0,
        ),
        name="products",
    )(slot_totals, place, sums, cooccur, *pieces)


def column_sum(value):
    size = lax.axis_size("col")
    step = size // 2
    while step:
        moves = [(index, index ^ step) for index in range(size)]
        value = value + lax.ppermute(value, "col", moves)
        step //= 2
    return value


def exchange(own, own_sums, sums):
    tiles = own.shape[1] // TILE
    half = tiles // 2
    first, last = (3 * tiles) // 8, (5 * tiles) // 8

    def cut(value, start, stop):
        return value[:, start * TILE : stop * TILE]

    left = send(own, 1, 0)
    right = send(own, -1, 0)
    across = send(own, 0, 1)
    slot_sums = column_sum(own_sums)
    left, right, across, slot_sums = lax.optimization_barrier((left, right, across, slot_sums))
    slot_totals = gathered(slot_sums, "row")
    near = jnp.concatenate([left, right, across], axis=0)
    low = jnp.concatenate([cut(left, 0, half), cut(across, 0, half)], axis=0)
    high = jnp.concatenate([cut(right, half, tiles), cut(across, half, tiles)], axis=0)
    turn = jnp.concatenate([cut(left, half, tiles), cut(right, 0, half)], axis=0)
    low = send(low, 1, 0)
    high = send(high, -1, 0)
    turn = send(turn, 0, 1)
    low, high, turn, slot_totals, sums = lax.optimization_barrier(
        (low, high, turn, slot_totals, sums)
    )
    middle = jnp.concatenate(
        [low, turn[SLOTS:], high[:SLOTS], turn[:SLOTS], high[SLOTS:]], axis=0
    )
    center = jnp.concatenate(
        [low[:SLOTS, first * TILE :], high[:SLOTS, : (last - half) * TILE]], axis=1
    )
    beyond = jnp.concatenate(
        [
            send(low[SLOTS:, : first * TILE], 1, 0),
            send(center, 0, 1),
            send(high[SLOTS:, (last - half) * TILE :], -1, 0),
        ],
        axis=1,
    )
    pieces = [own, near, beyond, middle]
    pieces = pieces + [send(piece, 0, 0, 1) for piece in pieces]
    return pieces, slot_totals, sums


def gathered(value, axis):
    size = lax.axis_size(axis)
    return lax.all_to_all(jnp.broadcast_to(value[None], (size,) + value.shape), axis, 0, 0)


def finish(shares):
    parts = lax.axis_size("col")
    shares = lax.all_to_all(shares, "col", 0, 0)
    end = shares.shape[1] - EXTRA
    gram_share = jnp.sum(shares[:, end - ANCHORS // parts : end, :], axis=0)
    return hals(shares, gathered(gram_share, "col"))


def quick(cooccur, anchors, owner, rank):
    rows = cooccur.shape[0]
    me = lax.axis_index("row")
    mine = (owner == me)[None, :] & (rank[None, :] == jnp.arange(SLOTS)[:, None])
    local = jnp.sum(jnp.where(mine, (anchors % rows)[None, :], 0), axis=1)
    own, own_sums = pick(cooccur, local)
    sums = jnp.sum(cooccur, axis=1, dtype=jnp.float32).reshape(lax.axis_size("col"), -1)
    pieces, slot_totals, sums = exchange(own, own_sums[:, 0], sums)
    mx, my, mc = me // (YS * CORES), me // CORES % YS, me % CORES
    absolute = jnp.stack(
        [
            (((mx - dx) % XS) * YS + (my ^ dy)) * CORES + (mc ^ dc)
            for dc in range(CORES)
            for dx, dy in SHIFTS
        ]
    )
    picked = absolute[:, None] == jnp.arange(SOURCES)[None, :]
    slot_totals = jnp.sum(jnp.where(picked[:, :, None], slot_totals[None], 0.0), axis=1)
    found = absolute[None, :] == owner[:, None]
    place = jnp.sum(jnp.where(found, jnp.arange(SOURCES)[None, :], 0), axis=1) * SLOTS + rank
    shares = products(
        cooccur,
        pieces,
        slot_totals.reshape(1, -1),
        place[:, None].astype(jnp.int32),
        sums,
    )
    return finish(shares)


def general(cooccur, anchors, owner):
    rows = cooccur.shape[0]
    parts = lax.axis_size("col")
    inside = owner == lax.axis_index("row")
    local = jnp.where(inside, anchors % rows, 0)
    picked = jnp.take(cooccur, local, axis=0)
    payload = jnp.where(inside[:, None], picked, jnp.zeros_like(picked))
    payload = payload.reshape(SOURCES, ANCHORS // SOURCES, -1)
    kept = jnp.sum(lax.all_to_all(payload, "row", 0, 0).astype(jnp.float32), axis=0)
    raw = gathered(kept.astype(jnp.bfloat16), "row").reshape(ANCHORS, -1).astype(jnp.float32)
    scale = column_sum(jnp.sum(raw, axis=1))
    basis = (raw / scale[:, None]).astype(jnp.bfloat16)
    gram = jnp.dot(basis, basis.T, preferred_element_type=jnp.float32)
    proj = jnp.dot(cooccur, basis.T, preferred_element_type=jnp.float32)
    totals = jnp.sum(cooccur, axis=1, dtype=jnp.float32).reshape(parts, 1, rows // parts)
    totals = jnp.broadcast_to(totals, (parts, EXTRA, rows // parts))
    totals = jnp.tile(totals, (1, 1, ANCHORS * parts // rows))
    proj = proj.reshape(parts, rows // parts, ANCHORS)
    gram = gram.reshape(parts, ANCHORS // parts, ANCHORS)
    return finish(jnp.concatenate([proj, gram, totals], axis=1))


def per_device(cooccur, anchors):
    rows = cooccur.shape[0]
    owner = anchors // rows
    earlier = jnp.arange(ANCHORS)[None, :] < jnp.arange(ANCHORS)[:, None]
    rank = jnp.sum((owner[:, None] == owner[None, :]) & earlier, axis=1)
    weights = quick(cooccur, anchors, owner, rank)

    def again(state):
        return jnp.array(False), general(cooccur, anchors, owner)

    overflow = jnp.max(rank) >= SLOTS
    return lax.while_loop(lambda state: state[0], again, (overflow, weights))[1]


def solution(mesh):
    placed = (P("row", "col"), P())
    return jax.shard_map(
        per_device, mesh=mesh, in_specs=placed, out_specs=P(None, ("row", "col")), check_vma=False
    )
```

```python
import jax
import jax.numpy as jnp
from jax import lax
from jax.experimental import pallas as pl
from jax.experimental.pallas import tpu as pltpu
from jax.sharding import PartitionSpec as P

ANCHORS = 256
BLOCK = 32
SWEEPS = 2
BLOCKS = ANCHORS // BLOCK
TILE = 1024
WIDE = 2048
SLOTS = 32
XS, YS, CORES = 4, 2, 2
SOURCES = XS * YS * CORES
SHIFTS = [(0, 0), (1, 0), (-1, 0), (0, 1), (2, 1), (2, 0), (1, 1), (-1, 1)]
GROUP = 8
EXTRA = 8
CONTRACT = (((1,), (1,)), ((), ()))


def shifted(dx, dy, dc):
    moves = []
    for x in range(XS):
        for y in range(YS):
            for c in range(CORES):
                source = (x * YS + y) * CORES + c
                target = (((x + dx) % XS) * YS + (y ^ dy)) * CORES + (c ^ dc)
                moves.append((source, target))
    return moves


def send(value, dx, dy, dc=0):
    return lax.ppermute(value, "row", shifted(dx, dy, dc))


def spread_row(ref, row):
    return ref[pl.ds(row, 8, stride=0), :]


def hals_kernel(share_ref, gram_in_ref, out_ref, gram_ref, target, coef, ratio, work, inverse):
    words = out_ref.shape[1]
    gram_ref[...] = gram_in_ref[...].reshape(ANCHORS, ANCHORS)
    share = jnp.sum(share_ref[...], axis=0)
    last = share.shape[0] - 1
    target[...] = share[:words, :].T / share[last:, :words]
    coef[...] = jnp.full_like(coef, 1.0 / ANCHORS)
    row_id = lax.broadcasted_iota(jnp.int32, (BLOCK, BLOCK), 0)
    col_id = lax.broadcasted_iota(jnp.int32, (BLOCK, BLOCK), 1)
    for block in range(BLOCKS):
        start = block * BLOCK
        square = gram_ref[start : start + BLOCK, start : start + BLOCK]
        diagonal = jnp.sum(jnp.where(row_id == col_id, square, 0.0), axis=1, keepdims=True)
        inv = 1.0 / diagonal
        inverse[start : start + BLOCK, :] = jnp.broadcast_to(inv, (BLOCK, words))
        scaled = square * inv
        for j in range(BLOCK):
            first = start * BLOCK + j * BLOCK
            ratio[first : first + BLOCK, :] = jnp.broadcast_to(
                scaled[:, j : j + 1], (BLOCK, words)
            )

    def step(index, carry):
        block = lax.rem(index, BLOCKS)
        start = pl.multiple_of(block * BLOCK, BLOCK)
        rows = pl.ds(start, BLOCK)
        moved = jnp.dot(
            gram_ref[rows, :],
            coef[...],
            precision=lax.Precision.HIGHEST,
            preferred_element_type=jnp.float32,
        )
        work[...] = (target[rows, :] - moved) * inverse[rows, :]
        resid = [spread_row(work, m) for m in range(BLOCK)]
        base = start * BLOCK
        for j in range(BLOCK):
            old = spread_row(coef, start + j)
            delta = jnp.maximum(resid[j], -old)
            coef[pl.ds(start + j, 1), :] = (old + delta)[0:1, :]
            for m in range(j + 1, BLOCK):
                resid[m] = resid[m] - spread_row(ratio, base + j * BLOCK + m) * delta
        return carry

    lax.fori_loop(0, SWEEPS * BLOCKS, step, 0)
    out_ref[...] = ANCHORS * coef[...]


def hals(shares, gram):
    words = shares.shape[1] - EXTRA - gram.shape[1]
    return pl.pallas_call(
        hals_kernel,
        out_shape=jax.ShapeDtypeStruct((ANCHORS, words), jnp.float32),
        scratch_shapes=[
            pltpu.VMEM((ANCHORS, ANCHORS), jnp.float32),
            pltpu.VMEM((ANCHORS, words), jnp.float32),
            pltpu.VMEM((ANCHORS, words), jnp.float32),
            pltpu.VMEM((ANCHORS * BLOCK, words), jnp.float32),
            pltpu.VMEM((BLOCK, words), jnp.float32),
            pltpu.VMEM((ANCHORS, words), jnp.float32),
        ],
        compiler_params=pltpu.CompilerParams(vmem_limit_bytes=32 << 20),
        name="hals",
    )(shares, gram)


def pick_kernel(group_ref, spot_ref, block_ref, own_ref, sums_ref, held, sems):
    columns = block_ref.shape[1]
    copies = []
    for slot in range(SLOTS):
        first = pl.multiple_of(group_ref[slot] * GROUP, GROUP)
        copies.append(
            pltpu.make_async_copy(
                block_ref.at[pl.ds(first, GROUP), :],
                held.at[pl.ds(slot * GROUP, GROUP), :],
                sems.at[slot],
            )
        )
        copies[-1].start()
    row = lax.broadcasted_iota(jnp.int32, (SLOTS, SLOTS * GROUP), 1)
    select = (row == spot_ref[...]).astype(jnp.float32).astype(jnp.bfloat16)
    for copy in copies:
        copy.wait()
    sums = jnp.zeros((SLOTS, 1), jnp.float32)
    for start in range(0, columns, TILE):
        rows = jnp.dot(
            select, held[:, start : start + TILE], preferred_element_type=jnp.float32
        )
        own_ref[:, start : start + TILE] = rows.astype(jnp.bfloat16)
        sums = sums + jnp.sum(rows, axis=1, keepdims=True)
    sums_ref[...] = sums


def pick(cooccur, local):
    columns = cooccur.shape[1]
    spot = jnp.arange(SLOTS) * GROUP + local % GROUP
    return pl.pallas_call(
        pick_kernel,
        grid_spec=pltpu.PrefetchScalarGridSpec(
            num_scalar_prefetch=1,
            grid=(1,),
            in_specs=[
                pl.BlockSpec((SLOTS, 1), lambda i, g: (0, 0)),
                pl.BlockSpec(memory_space=pltpu.HBM),
            ],
            out_specs=[
                pl.BlockSpec((SLOTS, columns), lambda i, g: (0, 0)),
                pl.BlockSpec((SLOTS, 1), lambda i, g: (0, 0)),
            ],
            scratch_shapes=[
                pltpu.VMEM((SLOTS * GROUP, columns), jnp.bfloat16),
                pltpu.SemaphoreType.DMA((SLOTS,)),
            ],
        ),
        out_shape=[
            jax.ShapeDtypeStruct((SLOTS, columns), jnp.bfloat16),
            jax.ShapeDtypeStruct((SLOTS, 1), jnp.float32),
        ],
        compiler_params=pltpu.CompilerParams(vmem_limit_bytes=24 << 20),
        cost_estimate=pl.CostEstimate(
            flops=0, bytes_accessed=SLOTS * GROUP * columns * 2, transcendentals=0
        ),
        name="pick",
    )((local // GROUP).astype(jnp.int32), spot[:, None].astype(jnp.int32), cooccur)


def wanted(tile, tiles):
    found = []
    for core in range(CORES):
        own, near, beyond, low, high, turn = range(6 * core, 6 * core + 6)
        base = core * len(SHIFTS) * SLOTS
        found += [(own, 0, SLOTS, base), (near, 0, 3 * SLOTS, base + SLOTS)]
        found += [(beyond, 0, SLOTS, base + 4 * SLOTS)]
        if tile < tiles // 2:
            found += [(low, 0, 2 * SLOTS, base + 5 * SLOTS), (turn, SLOTS, SLOTS, base + 7 * SLOTS)]
        else:
            found += [(high, 0, SLOTS, base + 5 * SLOTS), (turn, 0, SLOTS, base + 6 * SLOTS)]
            found += [(high, SLOTS, SLOTS, base + 7 * SLOTS)]
    return found


def products_kernel(totals_ref, place_ref, sums_ref, block_ref, *rest):
    piece_count = len(rest) - 7
    pieces = rest[:piece_count]
    out_ref, held, block, proj, gram_sum, held_sems, block_sems = rest[piece_count:]
    tiles = held.shape[0]
    parts, rows = out_ref.shape[0], out_ref.shape[1] - EXTRA
    gram_rows = ANCHORS // parts
    rows -= gram_rows
    found, fetched = [], []
    for tile in range(tiles):
        for index, (piece, first, size, start) in enumerate(wanted(tile, tiles)):
            column = tile * WIDE % pieces[piece].shape[1]
            found.append(
                pltpu.make_async_copy(
                    pieces[piece].at[pl.ds(first, size), pl.ds(column, WIDE)],
                    held.at[tile, pl.ds(start, size), :],
                    held_sems.at[tile, index],
                )
            )
            found[-1].start()
        fetched.append(
            pltpu.make_async_copy(
                block_ref.at[:, pl.ds(tile * WIDE, WIDE)], block.at[tile], block_sems.at[tile]
            )
        )
        fetched[-1].start()
    slot = lax.broadcasted_iota(jnp.int32, (ANCHORS, SOURCES * SLOTS), 1)
    chosen = slot == place_ref[...]
    select = chosen.astype(jnp.float32).astype(jnp.bfloat16)
    scale = 1.0 / jnp.sum(jnp.where(chosen, totals_ref[...], 0.0), axis=1, keepdims=True)
    waited = 0
    for tile in range(tiles):
        for _ in wanted(tile, tiles):
            found[waited].wait()
            waited += 1
        raw = jnp.dot(select, held[tile], preferred_element_type=jnp.float32)
        basis = (raw * scale).astype(jnp.bfloat16)
        gram = lax.dot_general(basis, basis, CONTRACT, preferred_element_type=jnp.float32)
        fetched[tile].wait()
        product = lax.dot_general(
            block[tile], basis, CONTRACT, preferred_element_type=jnp.float32
        )
        if tile == 0:
            gram_sum[...] = gram
            proj[...] = product
        else:
            gram_sum[...] += gram
            proj[...] += product
    for part in range(parts):
        out_ref[part, :rows, :] = proj[part * rows : (part + 1) * rows, :]
        out_ref[part, rows : rows + gram_rows, :] = gram_sum[
            part * gram_rows : (part + 1) * gram_rows, :
        ]
        row = jnp.concatenate([sums_ref[part : part + 1, :]] * (ANCHORS // rows), axis=1)
        out_ref[part, rows + gram_rows :, :] = jnp.broadcast_to(row, (EXTRA, ANCHORS))


def products(cooccur, pieces, slot_totals, place, sums):
    rows, columns = cooccur.shape
    parts = sums.shape[0]
    tiles = columns // WIDE
    return pl.pallas_call(
        products_kernel,
        in_specs=[pl.BlockSpec(memory_space=pltpu.VMEM)] * 3
        + [pl.BlockSpec(memory_space=pltpu.HBM)] * (1 + len(pieces)),
        out_specs=pl.BlockSpec(memory_space=pltpu.VMEM),
        out_shape=jax.ShapeDtypeStruct(
            (parts, (rows + ANCHORS) // parts + EXTRA, ANCHORS), jnp.float32
        ),
        scratch_shapes=[
            pltpu.VMEM((tiles, SOURCES * SLOTS, WIDE), jnp.bfloat16),
            pltpu.VMEM((tiles, rows, WIDE), jnp.bfloat16),
            pltpu.VMEM((rows, ANCHORS), jnp.float32),
            pltpu.VMEM((ANCHORS, ANCHORS), jnp.float32),
            pltpu.SemaphoreType.DMA((tiles, len(pieces))),
            pltpu.SemaphoreType.DMA((tiles,)),
        ],
        compiler_params=pltpu.CompilerParams(vmem_limit_bytes=52 << 20),
        cost_estimate=pl.CostEstimate(
            flops=2 * ANCHORS * (SOURCES * SLOTS + ANCHORS + rows) * columns,
            bytes_accessed=(SOURCES * SLOTS + rows) * columns * 2,
            transcendentals=0,
        ),
        name="products",
    )(slot_totals, place, sums, cooccur, *pieces)


def column_sum(value):
    size = lax.axis_size("col")
    step = size // 2
    while step:
        moves = [(index, index ^ step) for index in range(size)]
        value = value + lax.ppermute(value, "col", moves)
        step //= 2
    return value


def exchange(own, own_sums, sums):
    tiles = own.shape[1] // TILE
    half = tiles // 2
    first, last = (3 * tiles) // 8, (5 * tiles) // 8

    def cut(value, start, stop):
        return value[:, start * TILE : stop * TILE]

    left = send(own, 1, 0)
    right = send(own, -1, 0)
    across = send(own, 0, 1)
    left, right, across, own_sums, sums = lax.optimization_barrier(
        (left, right, across, own_sums, sums)
    )
    near = jnp.concatenate([left, right, across], axis=0)
    low = jnp.concatenate([cut(left, 0, half), cut(across, 0, half)], axis=0)
    high = jnp.concatenate([cut(right, half, tiles), cut(across, half, tiles)], axis=0)
    turn = jnp.concatenate([cut(left, half, tiles), cut(right, 0, half)], axis=0)
    low = send(low, 1, 0)
    high = send(high, -1, 0)
    turn = send(turn, 0, 1)
    slot_sums = column_sum(own_sums)
    low, high, turn, slot_sums = lax.optimization_barrier((low, high, turn, slot_sums))
    slot_totals = gathered(slot_sums, "row")
    center = jnp.concatenate(
        [low[:SLOTS, first * TILE :], high[:SLOTS, : (last - half) * TILE]], axis=1
    )
    beyond = jnp.concatenate(
        [
            send(low[SLOTS:, : first * TILE], 1, 0),
            send(center, 0, 1),
            send(high[SLOTS:, (last - half) * TILE :], -1, 0),
        ],
        axis=1,
    )
    beyond, slot_totals = lax.optimization_barrier((beyond, slot_totals))
    pieces = [own, near, beyond, low, high, turn]
    pieces = pieces + [send(piece, 0, 0, 1) for piece in pieces]
    return pieces, slot_totals, sums


def gathered(value, axis):
    size = lax.axis_size(axis)
    return lax.all_to_all(jnp.broadcast_to(value[None], (size,) + value.shape), axis, 0, 0)


def finish(shares):
    parts = lax.axis_size("col")
    shares = lax.all_to_all(shares, "col", 0, 0)
    end = shares.shape[1] - EXTRA
    gram_share = jnp.sum(shares[:, end - ANCHORS // parts : end, :], axis=0)
    return hals(shares, gathered(gram_share, "col"))


def quick(cooccur, anchors, owner, rank):
    rows = cooccur.shape[0]
    me = lax.axis_index("row")
    mine = (owner == me)[None, :] & (rank[None, :] == jnp.arange(SLOTS)[:, None])
    local = jnp.sum(jnp.where(mine, (anchors % rows)[None, :], 0), axis=1)
    own, own_sums = pick(cooccur, local)
    sums = jnp.sum(cooccur, axis=1, dtype=jnp.float32).reshape(lax.axis_size("col"), -1)
    pieces, slot_totals, sums = exchange(own, own_sums[:, 0], sums)
    mx, my, mc = me // (YS * CORES), me // CORES % YS, me % CORES
    absolute = jnp.stack(
        [
            (((mx - dx) % XS) * YS + (my ^ dy)) * CORES + (mc ^ dc)
            for dc in range(CORES)
            for dx, dy in SHIFTS
        ]
    )
    picked = absolute[:, None] == jnp.arange(SOURCES)[None, :]
    slot_totals = jnp.sum(jnp.where(picked[:, :, None], slot_totals[None], 0.0), axis=1)
    found = absolute[None, :] == owner[:, None]
    place = jnp.sum(jnp.where(found, jnp.arange(SOURCES)[None, :], 0), axis=1) * SLOTS + rank
    shares = products(
        cooccur,
        pieces,
        slot_totals.reshape(1, -1),
        place[:, None].astype(jnp.int32),
        sums,
    )
    return finish(shares)


def general(cooccur, anchors, owner):
    rows = cooccur.shape[0]
    parts = lax.axis_size("col")
    inside = owner == lax.axis_index("row")
    local = jnp.where(inside, anchors % rows, 0)
    picked = jnp.take(cooccur, local, axis=0)
    payload = jnp.where(inside[:, None], picked, jnp.zeros_like(picked))
    payload = payload.reshape(SOURCES, ANCHORS // SOURCES, -1)
    kept = jnp.sum(lax.all_to_all(payload, "row", 0, 0).astype(jnp.float32), axis=0)
    raw = gathered(kept.astype(jnp.bfloat16), "row").reshape(ANCHORS, -1).astype(jnp.float32)
    scale = column_sum(jnp.sum(raw, axis=1))
    basis = (raw / scale[:, None]).astype(jnp.bfloat16)
    gram = jnp.dot(basis, basis.T, preferred_element_type=jnp.float32)
    proj = jnp.dot(cooccur, basis.T, preferred_element_type=jnp.float32)
    totals = jnp.sum(cooccur, axis=1, dtype=jnp.float32).reshape(parts, 1, rows // parts)
    totals = jnp.broadcast_to(totals, (parts, EXTRA, rows // parts))
    totals = jnp.tile(totals, (1, 1, ANCHORS * parts // rows))
    proj = proj.reshape(parts, rows // parts, ANCHORS)
    gram = gram.reshape(parts, ANCHORS // parts, ANCHORS)
    return finish(jnp.concatenate([proj, gram, totals], axis=1))


def per_device(cooccur, anchors):
    rows = cooccur.shape[0]
    owner = anchors // rows
    earlier = jnp.arange(ANCHORS)[None, :] < jnp.arange(ANCHORS)[:, None]
    rank = jnp.sum((owner[:, None] == owner[None, :]) & earlier, axis=1)
    weights = quick(cooccur, anchors, owner, rank)

    def again(state):
        return jnp.array(False), general(cooccur, anchors, owner)

    overflow = jnp.max(rank) >= SLOTS
    return lax.while_loop(lambda state: state[0], again, (overflow, weights))[1]


def solution(mesh):
    placed = (P("row", "col"), P())
    return jax.shard_map(
        per_device, mesh=mesh, in_specs=placed, out_specs=P(None, ("row", "col")), check_vma=False
    )
```

```python
import jax
import jax.numpy as jnp
from jax import lax
from jax.experimental import pallas as pl
from jax.experimental.pallas import tpu as pltpu
from jax.sharding import PartitionSpec as P

ANCHORS = 256
BLOCK = 32
SWEEPS = 2
BLOCKS = ANCHORS // BLOCK
TILE = 1024
WIDE = 2048
SLOTS = 32
XS, YS, CORES = 4, 2, 2
SOURCES = XS * YS * CORES
SHIFTS = [(0, 0), (1, 0), (-1, 0), (0, 1), (2, 1), (2, 0), (1, 1), (-1, 1)]
GROUP = 8
EXTRA = 8
CONTRACT = (((1,), (1,)), ((), ()))


def shifted(dx, dy, dc):
    moves = []
    for x in range(XS):
        for y in range(YS):
            for c in range(CORES):
                source = (x * YS + y) * CORES + c
                target = (((x + dx) % XS) * YS + (y ^ dy)) * CORES + (c ^ dc)
                moves.append((source, target))
    return moves


def send(value, dx, dy, dc=0):
    return lax.ppermute(value, "row", shifted(dx, dy, dc))


def spread_row(ref, row):
    return ref[pl.ds(row, 8, stride=0), :]


def hals_kernel(share_ref, gram_in_ref, out_ref, gram_ref, target, coef, ratio, work, inverse):
    words = out_ref.shape[1]
    gram_ref[...] = gram_in_ref[...].reshape(ANCHORS, ANCHORS)
    share = jnp.sum(share_ref[...], axis=0)
    last = share.shape[0] - 1
    target[...] = share[:words, :].T / share[last:, :words]
    coef[...] = jnp.full_like(coef, 1.0 / ANCHORS)
    row_id = lax.broadcasted_iota(jnp.int32, (BLOCK, BLOCK), 0)
    col_id = lax.broadcasted_iota(jnp.int32, (BLOCK, BLOCK), 1)
    for block in range(BLOCKS):
        start = block * BLOCK
        square = gram_ref[start : start + BLOCK, start : start + BLOCK]
        diagonal = jnp.sum(jnp.where(row_id == col_id, square, 0.0), axis=1, keepdims=True)
        inv = 1.0 / diagonal
        inverse[start : start + BLOCK, :] = jnp.broadcast_to(inv, (BLOCK, words))
        scaled = square * inv
        for j in range(BLOCK):
            first = start * BLOCK + j * BLOCK
            ratio[first : first + BLOCK, :] = jnp.broadcast_to(
                scaled[:, j : j + 1], (BLOCK, words)
            )

    def step(index, carry):
        block = lax.rem(index, BLOCKS)
        start = pl.multiple_of(block * BLOCK, BLOCK)
        rows = pl.ds(start, BLOCK)
        moved = jnp.dot(
            gram_ref[rows, :],
            coef[...],
            precision=lax.Precision.HIGHEST,
            preferred_element_type=jnp.float32,
        )
        work[...] = (target[rows, :] - moved) * inverse[rows, :]
        resid = [spread_row(work, m) for m in range(BLOCK)]
        base = start * BLOCK
        for j in range(BLOCK):
            old = spread_row(coef, start + j)
            delta = jnp.maximum(resid[j], -old)
            coef[pl.ds(start + j, 1), :] = (old + delta)[0:1, :]
            for m in range(j + 1, BLOCK):
                resid[m] = resid[m] - spread_row(ratio, base + j * BLOCK + m) * delta
        return carry

    lax.fori_loop(0, SWEEPS * BLOCKS, step, 0)
    out_ref[...] = ANCHORS * coef[...]


def hals(shares, gram):
    words = shares.shape[1] - EXTRA - gram.shape[1]
    return pl.pallas_call(
        hals_kernel,
        out_shape=jax.ShapeDtypeStruct((ANCHORS, words), jnp.float32),
        scratch_shapes=[
            pltpu.VMEM((ANCHORS, ANCHORS), jnp.float32),
            pltpu.VMEM((ANCHORS, words), jnp.float32),
            pltpu.VMEM((ANCHORS, words), jnp.float32),
            pltpu.VMEM((ANCHORS * BLOCK, words), jnp.float32),
            pltpu.VMEM((BLOCK, words), jnp.float32),
            pltpu.VMEM((ANCHORS, words), jnp.float32),
        ],
        compiler_params=pltpu.CompilerParams(vmem_limit_bytes=32 << 20),
        name="hals",
    )(shares, gram)


def pick_kernel(group_ref, spot_ref, block_ref, own_ref, sums_ref, held, sems):
    columns = block_ref.shape[1]
    copies = []
    for slot in range(SLOTS):
        first = pl.multiple_of(group_ref[slot] * GROUP, GROUP)
        copies.append(
            pltpu.make_async_copy(
                block_ref.at[pl.ds(first, GROUP), :],
                held.at[pl.ds(slot * GROUP, GROUP), :],
                sems.at[slot],
            )
        )
        copies[-1].start()
    row = lax.broadcasted_iota(jnp.int32, (SLOTS, SLOTS * GROUP), 1)
    select = (row == spot_ref[...]).astype(jnp.float32).astype(jnp.bfloat16)
    for copy in copies:
        copy.wait()
    sums = jnp.zeros((SLOTS, 1), jnp.float32)
    for start in range(0, columns, TILE):
        rows = jnp.dot(
            select, held[:, start : start + TILE], preferred_element_type=jnp.float32
        )
        own_ref[:, start : start + TILE] = rows.astype(jnp.bfloat16)
        sums = sums + jnp.sum(rows, axis=1, keepdims=True)
    sums_ref[...] = sums


def pick(cooccur, local):
    columns = cooccur.shape[1]
    spot = jnp.arange(SLOTS) * GROUP + local % GROUP
    return pl.pallas_call(
        pick_kernel,
        grid_spec=pltpu.PrefetchScalarGridSpec(
            num_scalar_prefetch=1,
            grid=(1,),
            in_specs=[
                pl.BlockSpec((SLOTS, 1), lambda i, g: (0, 0)),
                pl.BlockSpec(memory_space=pltpu.HBM),
            ],
            out_specs=[
                pl.BlockSpec((SLOTS, columns), lambda i, g: (0, 0)),
                pl.BlockSpec((SLOTS, 1), lambda i, g: (0, 0)),
            ],
            scratch_shapes=[
                pltpu.VMEM((SLOTS * GROUP, columns), jnp.bfloat16),
                pltpu.SemaphoreType.DMA((SLOTS,)),
            ],
        ),
        out_shape=[
            jax.ShapeDtypeStruct((SLOTS, columns), jnp.bfloat16),
            jax.ShapeDtypeStruct((SLOTS, 1), jnp.float32),
        ],
        compiler_params=pltpu.CompilerParams(vmem_limit_bytes=24 << 20),
        cost_estimate=pl.CostEstimate(
            flops=0, bytes_accessed=SLOTS * GROUP * columns * 2, transcendentals=0
        ),
        name="pick",
    )((local // GROUP).astype(jnp.int32), spot[:, None].astype(jnp.int32), cooccur)


def wanted(tile, tiles):
    found = []
    for core in range(CORES):
        own, near, beyond, low, high, turn = range(6 * core, 6 * core + 6)
        base = core * len(SHIFTS) * SLOTS
        found += [(own, 0, SLOTS, base), (near, 0, 3 * SLOTS, base + SLOTS)]
        found += [(beyond, 0, SLOTS, base + 4 * SLOTS)]
        if tile < tiles // 2:
            found += [(low, 0, 2 * SLOTS, base + 5 * SLOTS), (turn, SLOTS, SLOTS, base + 7 * SLOTS)]
        else:
            found += [(high, 0, SLOTS, base + 5 * SLOTS), (turn, 0, SLOTS, base + 6 * SLOTS)]
            found += [(high, SLOTS, SLOTS, base + 7 * SLOTS)]
    return found


def products_kernel(totals_ref, place_ref, sums_ref, block_ref, *rest):
    piece_count = len(rest) - 7
    pieces = rest[:piece_count]
    out_ref, held, block, proj, gram_sum, held_sems, block_sems = rest[piece_count:]
    tiles = held.shape[0]
    parts, rows = out_ref.shape[0], out_ref.shape[1] - EXTRA
    gram_rows = ANCHORS // parts
    rows -= gram_rows
    found, fetched = [], []
    for tile in range(tiles):
        for index, (piece, first, size, start) in enumerate(wanted(tile, tiles)):
            column = tile * WIDE % pieces[piece].shape[1]
            found.append(
                pltpu.make_async_copy(
                    pieces[piece].at[pl.ds(first, size), pl.ds(column, WIDE)],
                    held.at[tile, pl.ds(start, size), :],
                    held_sems.at[tile, index],
                )
            )
            found[-1].start()
        fetched.append(
            pltpu.make_async_copy(
                block_ref.at[:, pl.ds(tile * WIDE, WIDE)], block.at[tile], block_sems.at[tile]
            )
        )
        fetched[-1].start()
    slot = lax.broadcasted_iota(jnp.int32, (ANCHORS, SOURCES * SLOTS), 1)
    chosen = slot == place_ref[...]
    select = chosen.astype(jnp.float32).astype(jnp.bfloat16)
    scale = 1.0 / jnp.sum(jnp.where(chosen, totals_ref[...], 0.0), axis=1, keepdims=True)
    waited = 0
    for tile in range(tiles):
        for _ in wanted(tile, tiles):
            found[waited].wait()
            waited += 1
        raw = jnp.dot(select, held[tile], preferred_element_type=jnp.float32)
        basis = (raw * scale).astype(jnp.bfloat16)
        gram = lax.dot_general(basis, basis, CONTRACT, preferred_element_type=jnp.float32)
        fetched[tile].wait()
        product = lax.dot_general(
            block[tile], basis, CONTRACT, preferred_element_type=jnp.float32
        )
        if tile == 0:
            gram_sum[...] = gram
            proj[...] = product
        else:
            gram_sum[...] += gram
            proj[...] += product
    for part in range(parts):
        out_ref[part, :rows, :] = proj[part * rows : (part + 1) * rows, :]
        out_ref[part, rows : rows + gram_rows, :] = gram_sum[
            part * gram_rows : (part + 1) * gram_rows, :
        ]
        row = jnp.concatenate([sums_ref[part : part + 1, :]] * (ANCHORS // rows), axis=1)
        out_ref[part, rows + gram_rows :, :] = jnp.broadcast_to(row, (EXTRA, ANCHORS))


def products(cooccur, pieces, slot_totals, place, sums):
    rows, columns = cooccur.shape
    parts = sums.shape[0]
    tiles = columns // WIDE
    return pl.pallas_call(
        products_kernel,
        in_specs=[pl.BlockSpec(memory_space=pltpu.VMEM)] * 3
        + [pl.BlockSpec(memory_space=pltpu.HBM)] * (1 + len(pieces)),
        out_specs=pl.BlockSpec(memory_space=pltpu.VMEM),
        out_shape=jax.ShapeDtypeStruct(
            (parts, (rows + ANCHORS) // parts + EXTRA, ANCHORS), jnp.float32
        ),
        scratch_shapes=[
            pltpu.VMEM((tiles, SOURCES * SLOTS, WIDE), jnp.bfloat16),
            pltpu.VMEM((tiles, rows, WIDE), jnp.bfloat16),
            pltpu.VMEM((rows, ANCHORS), jnp.float32),
            pltpu.VMEM((ANCHORS, ANCHORS), jnp.float32),
            pltpu.SemaphoreType.DMA((tiles, len(pieces))),
            pltpu.SemaphoreType.DMA((tiles,)),
        ],
        compiler_params=pltpu.CompilerParams(vmem_limit_bytes=52 << 20),
        cost_estimate=pl.CostEstimate(
            flops=2 * ANCHORS * (SOURCES * SLOTS + ANCHORS + rows) * columns,
            bytes_accessed=(SOURCES * SLOTS + rows) * columns * 2,
            transcendentals=0,
        ),
        name="products",
    )(slot_totals, place, sums, cooccur, *pieces)


def column_sum(value):
    size = lax.axis_size("col")
    step = size // 2
    while step:
        moves = [(index, index ^ step) for index in range(size)]
        value = value + lax.ppermute(value, "col", moves)
        step //= 2
    return value


def exchange(own, own_sums, sums):
    tiles = own.shape[1] // TILE
    half = tiles // 2
    first, last = (3 * tiles) // 8, (5 * tiles) // 8

    def cut(value, start, stop):
        return value[:, start * TILE : stop * TILE]

    left = send(own, 1, 0)
    right = send(own, -1, 0)
    across = send(own, 0, 1)
    left, right, across, own_sums, sums = lax.optimization_barrier(
        (left, right, across, own_sums, sums)
    )
    near = jnp.concatenate([left, right, across], axis=0)
    low = jnp.concatenate([cut(left, 0, half), cut(across, 0, half)], axis=0)
    high = jnp.concatenate([cut(right, half, tiles), cut(across, half, tiles)], axis=0)
    turn = jnp.concatenate([cut(left, half, tiles), cut(right, 0, half)], axis=0)
    low = send(low, 1, 0)
    high = send(high, -1, 0)
    turn = send(turn, 0, 1)
    slot_sums = column_sum(own_sums)
    slot_totals = gathered(slot_sums, "row")
    low, high, turn, slot_totals = lax.optimization_barrier((low, high, turn, slot_totals))
    center = jnp.concatenate(
        [low[:SLOTS, first * TILE :], high[:SLOTS, : (last - half) * TILE]], axis=1
    )
    beyond = jnp.concatenate(
        [
            send(low[SLOTS:, : first * TILE], 1, 0),
            send(center, 0, 1),
            send(high[SLOTS:, (last - half) * TILE :], -1, 0),
        ],
        axis=1,
    )
    pieces = [own, near, beyond, low, high, turn]
    pieces = pieces + [send(piece, 0, 0, 1) for piece in pieces]
    return pieces, slot_totals, sums


def gathered(value, axis):
    size = lax.axis_size(axis)
    return lax.all_to_all(jnp.broadcast_to(value[None], (size,) + value.shape), axis, 0, 0)


def finish(shares):
    parts = lax.axis_size("col")
    shares = lax.all_to_all(shares, "col", 0, 0)
    end = shares.shape[1] - EXTRA
    gram_share = jnp.sum(shares[:, end - ANCHORS // parts : end, :], axis=0)
    return hals(shares, gathered(gram_share, "col"))


def quick(cooccur, anchors, owner, rank):
    rows = cooccur.shape[0]
    me = lax.axis_index("row")
    mine = (owner == me)[None, :] & (rank[None, :] == jnp.arange(SLOTS)[:, None])
    local = jnp.sum(jnp.where(mine, (anchors % rows)[None, :], 0), axis=1)
    own, own_sums = pick(cooccur, local)
    sums = jnp.sum(cooccur, axis=1, dtype=jnp.float32).reshape(lax.axis_size("col"), -1)
    pieces, slot_totals, sums = exchange(own, own_sums[:, 0], sums)
    mx, my, mc = me // (YS * CORES), me // CORES % YS, me % CORES
    absolute = jnp.stack(
        [
            (((mx - dx) % XS) * YS + (my ^ dy)) * CORES + (mc ^ dc)
            for dc in range(CORES)
            for dx, dy in SHIFTS
        ]
    )
    picked = absolute[:, None] == jnp.arange(SOURCES)[None, :]
    slot_totals = jnp.sum(jnp.where(picked[:, :, None], slot_totals[None], 0.0), axis=1)
    found = absolute[None, :] == owner[:, None]
    place = jnp.sum(jnp.where(found, jnp.arange(SOURCES)[None, :], 0), axis=1) * SLOTS + rank
    shares = products(
        cooccur,
        pieces,
        slot_totals.reshape(1, -1),
        place[:, None].astype(jnp.int32),
        sums,
    )
    return finish(shares)


def general(cooccur, anchors, owner):
    rows = cooccur.shape[0]
    parts = lax.axis_size("col")
    inside = owner == lax.axis_index("row")
    local = jnp.where(inside, anchors % rows, 0)
    picked = jnp.take(cooccur, local, axis=0)
    payload = jnp.where(inside[:, None], picked, jnp.zeros_like(picked))
    payload = payload.reshape(SOURCES, ANCHORS // SOURCES, -1)
    kept = jnp.sum(lax.all_to_all(payload, "row", 0, 0).astype(jnp.float32), axis=0)
    raw = gathered(kept.astype(jnp.bfloat16), "row").reshape(ANCHORS, -1).astype(jnp.float32)
    scale = column_sum(jnp.sum(raw, axis=1))
    basis = (raw / scale[:, None]).astype(jnp.bfloat16)
    gram = jnp.dot(basis, basis.T, preferred_element_type=jnp.float32)
    proj = jnp.dot(cooccur, basis.T, preferred_element_type=jnp.float32)
    totals = jnp.sum(cooccur, axis=1, dtype=jnp.float32).reshape(parts, 1, rows // parts)
    totals = jnp.broadcast_to(totals, (parts, EXTRA, rows // parts))
    totals = jnp.tile(totals, (1, 1, ANCHORS * parts // rows))
    proj = proj.reshape(parts, rows // parts, ANCHORS)
    gram = gram.reshape(parts, ANCHORS // parts, ANCHORS)
    return finish(jnp.concatenate([proj, gram, totals], axis=1))


def per_device(cooccur, anchors):
    rows = cooccur.shape[0]
    owner = anchors // rows
    earlier = jnp.arange(ANCHORS)[None, :] < jnp.arange(ANCHORS)[:, None]
    rank = jnp.sum((owner[:, None] == owner[None, :]) & earlier, axis=1)
    weights = quick(cooccur, anchors, owner, rank)

    def again(state):
        return jnp.array(False), general(cooccur, anchors, owner)

    overflow = jnp.max(rank) >= SLOTS
    return lax.while_loop(lambda state: state[0], again, (overflow, weights))[1]


def solution(mesh):
    placed = (P("row", "col"), P())
    return jax.shard_map(
        per_device, mesh=mesh, in_specs=placed, out_specs=P(None, ("row", "col")), check_vma=False
    )
```
